32 devices in a mesh: dp: 8 (over z, core), vocab: 4 (over y, x).
Axes of the slice: x: 2, y: 2, z: 4, core: 2. Of those that a mesh axis runs over, the one named last changes fastest.
Arguments:
- hidden: float32 [16, 2, 32, 4096], P('dp', None, None, 'vocab'), may hold values from -64 to 64, as said below
- head_weight: float32 [4096, 1024], P(None, 'vocab'), may hold values from -1 to 1, as said below
- targets: int32 [16, 2, 32], P('dp'), may hold values from 0 to 1023
- lengths: int32 [16, 2], P('dp'), may hold values from 8 to 32
- rest_lse: float32 [16, 2, 32], P('dp'), may hold values from 6 to 10
- ref_logp: float32 [16, 2], P('dp'), may hold values from -120 to 120
- group_map: int32 [16], P('dp'), may hold values from 0 to 7, as said below
- group_weight: float32 [8], replicated, may hold values from 0.25 to 4
Outputs:
- hidden_grad: float32 [16, 2, 32, 4096], P('dp', None, None, 'vocab')
- dpo_loss: float32 [], replicated
The draws below stay inside these ranges and needn't reach their ends.
Inputs may be any that keep to these rules, and one draw needn't show every extreme that they name: `hidden`: standard normal states; in some draws a few tokens lie near large multiples of two head columns. `head_weight`: entries of order one over the square root of 4096. `group_map`: each pair names its own group or one of the two next to it (indices modulo 8); every group is named by exactly 2 pairs, and at most one pair of a group names each neighbour.
All inputs are finite; a program needn't handle non-finite values.
Results may differ from the reference program's by a relative error of at most 0.0003.
Values sent between devices are 32-bit elements; how exact they have to be, the bound alone decides.
A program may use at most 64 MiB of HBM per device.

```python
import math
import jax
import jax.numpy as jnp
import numpy as np
from jax import lax

D = 4096
SEQ = 32
PAIR_DEV = 2
WINDOW = 1024
PAIRS = 16
GROUPS = 8


def shared_draw(key):
    weight_key = jax.random.fold_in(key, 11)
    state_key = jax.random.fold_in(key, 12)
    weight = jax.random.truncated_normal(weight_key, -6.0, 6.0, (D, WINDOW), jnp.float32) / jnp.sqrt(jnp.float32(D))
    states = jax.random.truncated_normal(state_key, -6.0, 6.0, (PAIRS, 2, SEQ, D), jnp.float32)
    return (weight, states)


def draw_hidden(key, part):
    return shared_draw(key)[1]


def draw_head_weight(key, part):
    return shared_draw(key)[0]


def draw_group_map(key, part):
    swap_key = jax.random.fold_in(key, 21)
    order_key = jax.random.fold_in(key, 22)
    swaps = jax.random.randint(swap_key, (GROUPS,), 0, 2)
    group_ids = lax.iota(jnp.int32, GROUPS)
    going_left = jnp.roll(swaps, 1)
    scores = jax.random.randint(order_key, (GROUPS, PAIR_DEV), 0, 1 << 20) * PAIR_DEV + lax.iota(jnp.int32, PAIR_DEV)[None, :]
    ranking = jnp.argsort(jnp.argsort(scores, axis=1), axis=1).astype(jnp.int32)
    to_left = ranking < going_left[:, None]
    to_right = (ranking >= going_left[:, None]) & (ranking < (going_left + swaps)[:, None])
    left_group = (group_ids + GROUPS - 1) % GROUPS
    right_group = (group_ids + 1) % GROUPS
    target_group = jnp.where(to_left, left_group[:, None], jnp.where(to_right, right_group[:, None], group_ids[:, None]))
    return target_group.reshape(GROUPS * PAIR_DEV).astype(jnp.int32)


def plant(values, key, low, high):
    spot = [jax.random.randint(jax.random.fold_in(key, axis), (), 0, length) for axis, length in enumerate(values.shape)]
    longest = values.shape.index(max(values.shape))
    neighbour = spot[:longest] + [(spot[longest] + 1) % values.shape[longest]] + spot[longest + 1:]
    return values.at[tuple(spot)].set(low).at[tuple(neighbour)].set(high)


def levels(key, dims, cuts, least, top_value):
    gain, own = 1.0, jax.random.fold_in(key, 6)
    for axis_at, parts in cuts:
        draws = jnp.exp(jax.random.uniform(jax.random.fold_in(own, axis_at), (parts,), jnp.float32, least / len(cuts), top_value / len(cuts)))
        gain = gain * jnp.repeat(draws, dims[axis_at] // parts).reshape([-1 if axis == axis_at else 1 for axis in range(len(dims))])
    return gain


def rank_bounds(amount, lean):
    loads = [(1 << 20) // math.isqrt(rank ** lean) + 1 for rank in range(1, amount + 1)]
    deviation = 1 + sum(loads) // (1 << 30)
    return np.cumsum(np.array([max(1, weight // deviation) for weight in loads]))


def ranked_ids(own_key, extent, amount, lean):
    table = rank_bounds(amount, lean)
    ticket = jax.random.randint(jax.random.fold_in(own_key, 1), extent, 0, int(table[amount - 1]))
    standing = jnp.searchsorted(jnp.asarray(table, jnp.int32), ticket, side="right")
    return jax.random.permutation(jax.random.fold_in(own_key, 2), amount)[standing].astype(jnp.int32)


def noise(own_key, shape, deviation, bound, shards=(), held_as=jnp.bfloat16):
    gain = levels(own_key, shape, shards, -0.22, 0.18) if shards else 1.0
    values = jax.random.normal(own_key, shape, jnp.float32) * deviation * gain
    return jnp.minimum(jnp.maximum(values, -bound), bound).astype(held_as)


def setup_inputs(seed: int = 0) -> dict:
    splits = jax.random.split(jax.random.key(seed), 9)
    return {
        "hidden": draw_hidden(jax.random.fold_in(splits[8], 71), 0),
        "head_weight": draw_head_weight(jax.random.fold_in(splits[8], 71), 0),
        "targets": plant(ranked_ids(splits[2], (PAIRS, 2, SEQ), WINDOW, 2), jax.random.fold_in(splits[2], 3), 0, WINDOW - 1).astype(jnp.int32),
        "lengths": plant(jax.random.randint(splits[3], (PAIRS, 2), SEQ // 4, SEQ + 1), jax.random.fold_in(splits[3], 1), SEQ // 4, SEQ).astype(jnp.int32),
        "rest_lse": jnp.clip(6.0 + 4.0 * jax.random.uniform(splits[4], (PAIRS, 2, SEQ), jnp.float32) ** levels(splits[4], (PAIRS, 2, SEQ), ((0, 8),), -0.2, 0.2), 6.0, 10.0),
        "ref_logp": noise(splits[5], (PAIRS, 2), 20.0, 120.0, ((0, 8),), jnp.float32),
        "group_map": draw_group_map(jax.random.fold_in(splits[8], 71), 0),
        "group_weight": jnp.clip(jnp.exp(jax.random.uniform(splits[7], (GROUPS,), jnp.float32, math.log(0.25), math.log(4.0))), 0.25, 4.0),
    }


beta_scale = 0.05
highest = lax.Precision.HIGHEST


def reference(hidden, head_weight, targets, lengths, rest_lse, ref_logp, group_map, group_weight):
    token_rows = hidden.reshape(PAIRS * 2 * SEQ, D)
    logits = jnp.dot(token_rows, head_weight, precision=highest, preferred_element_type=jnp.float32)
    row_peak = jnp.max(logits, axis=1)
    row_total = jnp.sum(jnp.exp(logits - row_peak[:, None]), axis=1)
    window_lse = row_peak + jnp.log(row_total)
    target_flat = targets.reshape(PAIRS * 2 * SEQ)
    matches = target_flat[:, None] == lax.iota(jnp.int32, WINDOW)[None, :]
    target_logit = jnp.sum(jnp.where(matches, logits, 0.0), axis=1)
    outside = rest_lse.reshape(PAIRS * 2 * SEQ)
    ceiling = jnp.maximum(window_lse, outside)
    full_lse = ceiling + jnp.log(jnp.exp(window_lse - ceiling) + jnp.exp(outside - ceiling))
    positions = lax.iota(jnp.int32, SEQ)
    live_tokens = (positions[None, None, :] < lengths[:, :, None]).astype(jnp.float32)
    token_logp = (target_logit - full_lse).reshape(PAIRS, 2, SEQ) * live_tokens
    sequence_logp = jnp.sum(token_logp, axis=2)
    margin = beta_scale * ((sequence_logp[:, 0] - ref_logp[:, 0]) - (sequence_logp[:, 1] - ref_logp[:, 1]))
    group_ids = lax.iota(jnp.int32, GROUPS)
    pair_weight = jnp.sum(jnp.where(group_map[:, None] == group_ids[None, :], group_weight[None, :], 0.0), axis=1)
    divisor = PAIR_DEV * jnp.sum(group_weight)
    dpo_loss = jnp.sum(pair_weight * jax.nn.softplus(-margin)) / divisor
    coefficient = -beta_scale * pair_weight * jax.nn.sigmoid(-margin) / divisor
    sign_pair = jnp.array([1.0, -1.0], jnp.float32)
    token_grad = (coefficient[:, None, None] * sign_pair[None, :, None] * live_tokens).reshape(PAIRS * 2 * SEQ)
    probability = jnp.exp(logits - full_lse[:, None])
    logit_grad = token_grad[:, None] * (matches.astype(jnp.float32) - probability)
    hidden_grad = jnp.dot(logit_grad, head_weight.T, precision=highest, preferred_element_type=jnp.float32)
    return hidden_grad.reshape(PAIRS, 2, SEQ, D), dpo_loss
```

```python
import functools

import jax
import jax.numpy as jnp
from jax import lax
from jax.experimental import pallas as pl
from jax.experimental.pallas import tpu as pltpu
from jax.sharding import PartitionSpec as P

beta_scale = 0.05
SHARE = 4
CHUNKS = 2
MESH = pl.DeviceIdType.MESH
f32, bf16 = jnp.float32, jnp.bfloat16
LANES = 128


def split(x):
    high = x.astype(bf16)
    return high, (x - high.astype(f32)).astype(bf16)


def kernel(n, m, hid, w, tgt, lens, rest, refl, gmap, gw, out, loss,
           hbuf, h2, wbuf, whi, wlo, plog, rbuf, gbuf, stat, lbuf,
           lsem, wsend, wrecv, zsend, zrecv, csend, crecv, rsend, rrecv, gsend, grecv, ssend, srecv, dsend, drecv):
    v, d = lax.axis_index("vocab"), lax.axis_index("dp")
    pairs, _, seq = tgt.shape
    tokens, rows = hid.shape
    cols = w.shape[1]
    groups = gw.shape[0]
    mine = tokens // n
    quarter = rows // SHARE
    chunk = quarter // CHUNKS
    share = d % SHARE
    partner = {"dp": d + 1 - 2 * (d % 2)}
    across = {"dp": d + 2 - 4 * ((d // 2) % 2)}
    across_share = (share + 2) % SHARE

    def peer(i):
        u, bit = v, 1
        while bit <= i:
            if i & bit:
                u = u + bit * (1 - 2 * ((v // bit) % 2))
            bit *= 2
        return u

    peers = [peer(i) for i in range(n)]

    def remote(src, dst, ss, rs, where):
        return pltpu.make_async_remote_copy(
            src_ref=src, dst_ref=dst, send_sem=ss, recv_sem=rs, device_id=where, device_id_type=MESH
        )

    barrier = pltpu.get_barrier_semaphore()
    for i in range(1, n):
        pl.semaphore_signal(barrier, inc=1, device_id={"vocab": peers[i]}, device_id_type=MESH)
    for j in range(1, m):
        pl.semaphore_signal(barrier, inc=1, device_id={"dp": (d + j) % m}, device_id_type=MESH)
    own_w = pltpu.make_async_copy(w.at[pl.ds(pl.multiple_of(v * rows, rows), rows), :], wbuf.at[v], lsem.at[0])
    own_h = pltpu.make_async_copy(hid, hbuf, lsem.at[1])
    own_w.start()
    own_h.start()
    pl.semaphore_wait(barrier, n + m - 2)

    order = sorted(
        ((i, c) for i in range(1, n) for c in range(CHUNKS)), key=lambda e: (bin(e[0]).count("1"), e[1], e[0])
    )

    def spot(part, c):
        return pl.ds(pl.multiple_of(part * quarter + c * chunk, chunk), chunk)

    def plane(i, c):
        start = pl.multiple_of(peers[i] * rows + share * quarter + c * chunk, chunk)
        return remote(w.at[pl.ds(start, chunk), :], wbuf.at[v, spot(share, c)],
                      wsend.at[i - 1, c], wrecv.at[i - 1, c], {"vocab": peers[i]})

    def along(i, c):
        here = wbuf.at[peers[i], spot(share, c)]
        return remote(here, here, zsend.at[i - 1, c], zrecv.at[i - 1, c], across)

    def beside(kind, i, c):
        here = wbuf.at[peers[i], spot(across_share if kind else share, c)]
        return remote(here, here, csend.at[kind, i - 1, c], crecv.at[kind, i - 1, c], partner)

    for i, c in order:
        plane(i, c).start()

    own_h.wait()
    high, low = split(hbuf[...])
    h2[pl.ds(0, tokens), :] = high
    h2[pl.ds(tokens, tokens), :] = low
    own_w.wait()

    def piece(u, i):
        return remote(plog.at[u, pl.ds(pl.multiple_of(peers[i] * mine, mine), mine), :], rbuf.at[i - 1, u],
                      rsend.at[i - 1], rrecv.at[i - 1], {"vocab": peers[i]})

    def forward(u):
        w_high, w_low = split(wbuf[u])
        whi[u] = w_high
        wlo[u] = w_low
        both = jnp.dot(h2[...], w_high, preferred_element_type=f32)
        rest_part = jnp.dot(h2[pl.ds(0, tokens), :], w_low, preferred_element_type=f32)
        plog[u] = both[:tokens] + both[tokens:] + rest_part
        for i in range(1, n):
            piece(u, i).start()

    forward(v)

    lag = 2
    waited = []
    total = len(order)
    for k in range(total + 2 * lag):
        if k < total:
            i, c = order[k]
            plane(i, c).wait_recv()
            along(i, c).start()
            beside(0, i, c).start()
        if lag <= k < total + lag:
            i, c = order[k - lag]
            along(i, c).wait_recv()
            beside(1, i, c).start()
        if k >= 2 * lag:
            i, c = order[k - 2 * lag]
            beside(0, i, c).wait_recv()
            beside(1, i, c).wait_recv()
            waited.append(i)
            if waited.count(i) == CHUNKS:
                forward(peers[i])

    token = v * mine + lax.broadcasted_iota(jnp.int32, (mine, 1), 0)
    lane_seq = lax.broadcasted_iota(jnp.int32, (mine, seq), 1)

    def column(ref):
        picked = jnp.zeros((mine, seq), f32)
        for p in range(pairs):
            for s in range(2):
                row = jnp.broadcast_to(ref[p, pl.ds(s, 1), :].astype(f32), (mine, seq))
                picked = jnp.where((token // seq == 2 * p + s) & (token % seq == lane_seq), row, picked)
        return jnp.sum(picked, axis=1, keepdims=True)

    target = column(tgt).astype(jnp.int32)
    outside = column(rest)
    length = jnp.zeros((mine, 1), jnp.int32)
    for p in range(pairs):
        for s in range(2):
            length = jnp.where(token // seq == 2 * p + s, lens[p, s], length)
    live = (token % seq < length).astype(f32)
    lane = lax.broadcasted_iota(jnp.int32, (mine, cols), 1)

    for i in range(1, n):
        remote(rbuf.at[i - 1], rbuf.at[i - 1], rsend.at[i - 1], rrecv.at[i - 1], {"vocab": peers[i]}).wait_recv()
    logits = []
    for u in range(n):
        block = plog[u, pl.ds(pl.multiple_of(v * mine, mine), mine), :]
        for i in range(1, n):
            block = block + rbuf[i - 1, u]
        logits.append(block)
    peak = functools.reduce(jnp.maximum, [jnp.max(b, axis=1, keepdims=True) for b in logits])
    row_total = sum(jnp.sum(jnp.exp(b - peak), axis=1, keepdims=True) for b in logits)
    matches = [target == u * cols + lane for u in range(n)]
    target_logit = sum(
        jnp.sum(jnp.where(k, b, 0.0), axis=1, keepdims=True) for k, b in zip(matches, logits)
    )
    window_lse = peak + jnp.log(row_total)
    ceiling = jnp.maximum(window_lse, outside)
    full_lse = ceiling + jnp.log(jnp.exp(window_lse - ceiling) + jnp.exp(outside - ceiling))
    stat[v] = jnp.broadcast_to((target_logit - full_lse) * live, (mine, LANES))
    for u in range(n):
        gbuf[u, v] = matches[u].astype(f32) - jnp.exp(logits[u] - full_lse)

    def share_stat(i):
        return remote(stat.at[v], stat.at[v], ssend.at[i - 1], srecv.at[i - 1], {"vocab": peers[i]})

    def share_grad(u, i):
        return remote(gbuf.at[u, v], gbuf.at[u, v], gsend.at[u, i - 1], grecv.at[u, i - 1], {"vocab": peers[i]})

    for i in range(1, n):
        share_stat(i).start()
    for u in range(n):
        for i in range(1, n):
            share_grad(u, i).start()

    for i in range(1, n):
        share_stat(i).wait_recv()
    divisor = pairs * sum(gw[g] for g in range(groups))
    position = lax.broadcasted_iota(jnp.int32, (seq, LANES), 0)
    per_token = stat[...].reshape(tokens, LANES)
    local_loss = jnp.zeros((1, LANES), f32)
    scales = []
    for p in range(pairs):
        weight = sum(jnp.where(gmap[p] == g, gw[g], 0.0) for g in range(groups))
        logp = [
            jnp.sum(per_token[(2 * p + s) * seq:(2 * p + s + 1) * seq], axis=0, keepdims=True) for s in range(2)
        ]
        margin = beta_scale * ((logp[0] - refl[p, 0]) - (logp[1] - refl[p, 1]))
        softplus = jnp.maximum(-margin, 0.0) + jnp.log1p(jnp.exp(-jnp.abs(margin)))
        local_loss = local_loss + weight * softplus
        falling = jnp.exp(-jnp.abs(margin))
        sigmoid = jnp.where(margin > 0.0, falling, 1.0) / (1.0 + falling)
        coefficient = -beta_scale * weight * sigmoid / jnp.full((1, LANES), divisor)
        for s in range(2):
            signed = coefficient if s == 0 else -coefficient
            scales.append(jnp.where(position < lens[p, s], jnp.broadcast_to(signed, (seq, LANES)), 0.0))
    lbuf[d] = jnp.broadcast_to(local_loss / jnp.full((1, LANES), divisor), (8, LANES))

    def share_loss(j):
        return remote(lbuf.at[d], lbuf.at[d], dsend, drecv, {"dp": (d + j) % m})

    for j in range(1, m):
        share_loss(j).start()

    contract = (((1,), (1,)), ((), ()))
    for u in range(n):
        for i in range(1, n):
            share_grad(u, i).wait_recv()
        high, low = split(gbuf[u].reshape(tokens, cols))
        part = lax.dot_general(jnp.concatenate([high, low], axis=0), whi[u], contract, preferred_element_type=f32)
        part = part[:tokens] + part[tokens:] + lax.dot_general(high, wlo[u], contract, preferred_element_type=f32)
        if u:
            part = part + out[...]
        if u == n - 1:
            part = part * jnp.concatenate(scales, axis=0)[:, :1]
        out[...] = part

    every_loss = remote(lbuf.at[pl.ds(0, m - 1)], lbuf.at[pl.ds(0, m - 1)], dsend, drecv, partner)
    every_loss.wait_recv()
    summed = lbuf[0]
    for j in range(1, m):
        summed = summed + lbuf[j]
    loss[0, 0] = summed[0, 0]

    for i, c in order:
        plane(i, c).wait_send()
        along(i, c).wait_send()
        beside(0, i, c).wait_send()
        beside(1, i, c).wait_send()
    for i in range(1, n):
        remote(rbuf.at[i - 1], rbuf.at[i - 1], rsend.at[i - 1], rrecv.at[i - 1], {"vocab": peers[i]}).wait_send()
        share_stat(i).wait_send()
        for u in range(n):
            share_grad(u, i).wait_send()
    every_loss.wait_send()


def solution(mesh):
    n, m = mesh.shape["vocab"], mesh.shape["dp"]

    def shards(hidden, head_weight, targets, lengths, rest_lse, ref_logp, group_map, group_weight):
        rows = hidden.shape[3]
        tokens = hidden.shape[0] * hidden.shape[1] * hidden.shape[2]
        cols = head_weight.shape[1]
        mine = tokens // n
        vmem, smem = pl.BlockSpec(memory_space=pltpu.VMEM), pl.BlockSpec(memory_space=pltpu.SMEM)
        hbm = pl.BlockSpec(memory_space=pl.ANY)
        dma = pltpu.SemaphoreType.DMA
        grad, loss = pl.pallas_call(
            functools.partial(kernel, n, m),
            out_shape=(jax.ShapeDtypeStruct((tokens, rows), f32), jax.ShapeDtypeStruct((1, 1), f32)),
            in_specs=[hbm, hbm, vmem, smem, vmem, smem, smem, smem],
            out_specs=(vmem, smem),
            scratch_shapes=[
                pltpu.VMEM((tokens, rows), f32),
                pltpu.VMEM((2 * tokens, rows), bf16),
                pltpu.VMEM((n, rows, cols), f32),
                pltpu.VMEM((n, rows, cols), bf16),
                pltpu.VMEM((n, rows, cols), bf16),
                pltpu.VMEM((n, tokens, cols), f32),
                pltpu.VMEM((n - 1, n, mine, cols), f32),
                pltpu.VMEM((n, n, mine, cols), f32),
                pltpu.VMEM((n, mine, LANES), f32),
                pltpu.VMEM((m, 8, LANES), f32),
                dma((2,)),
                dma((n - 1, CHUNKS)), dma((n - 1, CHUNKS)),
                dma((n - 1, CHUNKS)), dma((n - 1, CHUNKS)),
                dma((2, n - 1, CHUNKS)), dma((2, n - 1, CHUNKS)),
                dma((n - 1,)), dma((n - 1,)),
                dma((n, n - 1)), dma((n, n - 1)),
                dma((n - 1,)), dma((n - 1,)),
                dma, dma,
            ],
            compiler_params=pltpu.CompilerParams(
                collective_id=0, has_side_effects=True, vmem_limit_bytes=56 << 20
            ),
        )(hidden.reshape(tokens, rows), head_weight, targets, lengths, rest_lse, ref_logp, group_map, group_weight)
        return grad.reshape(hidden.shape), loss.reshape(())

    return jax.shard_map(
        shards,
        mesh=mesh,
        in_specs=(
            P("dp", None, None, "vocab"),
            P(None, "vocab"),
            P("dp", None, None),
            P("dp", None),
            P("dp", None, None),
            P("dp", None),
            P("dp"),
            P(),
        ),
        out_specs=(P("dp", None, None, "vocab"), P()),
        check_vma=False,
    )
```

```python
import functools

import jax
import jax.numpy as jnp
from jax import lax
from jax.experimental import pallas as pl
from jax.experimental.pallas import tpu as pltpu
from jax.sharding import PartitionSpec as P

beta_scale = 0.05
SHARE = 4
CHUNKS = 4
DIRECT = 2
MESH = pl.DeviceIdType.MESH
f32, bf16 = jnp.float32, jnp.bfloat16
LANES = 128


def split(x):
    high = x.astype(bf16)
    return high, (x - high.astype(f32)).astype(bf16)


def kernel(n, m, hid, w, tgt, lens, rest, refl, gmap, gw, out, loss,
           hbuf, h2, wbuf, whi, wlo, plog, rbuf, gbuf, stat, lbuf,
           lsem, wsend, wrecv, zsend, zrecv, csend, crecv, rsend, rrecv, gsend, grecv, ssend, srecv, dsend, drecv):
    v, d = lax.axis_index("vocab"), lax.axis_index("dp")
    pairs, _, seq = tgt.shape
    tokens, rows = hid.shape
    cols = w.shape[1]
    groups = gw.shape[0]
    mine = tokens // n
    quarter = rows // SHARE
    chunk = quarter // CHUNKS
    share = d % SHARE
    partner = {"dp": d + 1 - 2 * (d % 2)}
    across = {"dp": d + 2 - 4 * ((d // 2) % 2)}
    across_share = (share + 2) % SHARE

    def peer(i):
        u, bit = v, 1
        while bit <= i:
            if i & bit:
                u = u + bit * (1 - 2 * ((v // bit) % 2))
            bit *= 2
        return u

    peers = [peer(i) for i in range(n)]

    def remote(src, dst, ss, rs, where):
        return pltpu.make_async_remote_copy(
            src_ref=src, dst_ref=dst, send_sem=ss, recv_sem=rs, device_id=where, device_id_type=MESH
        )

    barrier = pltpu.get_barrier_semaphore()
    for i in range(1, n):
        pl.semaphore_signal(barrier, inc=1, device_id={"vocab": peers[i]}, device_id_type=MESH)
    for j in range(1, m):
        pl.semaphore_signal(barrier, inc=1, device_id={"dp": (d + j) % m}, device_id_type=MESH)
    own_w = pltpu.make_async_copy(w.at[pl.ds(pl.multiple_of(v * rows, rows), rows), :], wbuf.at[v], lsem.at[0])
    own_h = pltpu.make_async_copy(hid, hbuf, lsem.at[1])
    own_w.start()
    own_h.start()
    pl.semaphore_wait(barrier, n + m - 2)

    def hops(i):
        return bin(i).count("1")

    order = sorted(
        ((i, c) for i in range(1, n) for c in range(CHUNKS)), key=lambda e: (e[1] - hops(e[0]), -hops(e[0]), e[0])
    )

    def direct(i, c):
        return hops(i) == 1 and c >= CHUNKS - DIRECT

    def spot(part, c):
        return pl.ds(pl.multiple_of(part * quarter + c * chunk, chunk), chunk)

    def plane(i, c, part, ss, rs):
        start = pl.multiple_of(peers[i] * rows + part * quarter + c * chunk, chunk)
        return remote(w.at[pl.ds(start, chunk), :], wbuf.at[v, spot(part, c)],
                      ss.at[i - 1, c], rs.at[i - 1, c], {"vocab": peers[i]})

    def first(i, c):
        return plane(i, c, share, wsend, wrecv)

    def second(i, c):
        if direct(i, c):
            return plane(i, c, across_share, zsend, zrecv)
        here = wbuf.at[peers[i], spot(share, c)]
        return remote(here, here, zsend.at[i - 1, c], zrecv.at[i - 1, c], across)

    def beside(kind, i, c):
        here = wbuf.at[peers[i], spot(across_share if kind else share, c)]
        return remote(here, here, csend.at[kind, i - 1, c], crecv.at[kind, i - 1, c], partner)

    for i, c in order:
        first(i, c).start()
        if direct(i, c):
            second(i, c).start()

    own_h.wait()
    high, low = split(hbuf[...])
    h2[pl.ds(0, tokens), :] = high
    h2[pl.ds(tokens, tokens), :] = low
    own_w.wait()

    def piece(u, i):
        return remote(plog.at[u, pl.ds(pl.multiple_of(peers[i] * mine, mine), mine), :], rbuf.at[i - 1, u],
                      rsend.at[i - 1], rrecv.at[i - 1], {"vocab": peers[i]})

    def forward(u):
        w_high, w_low = split(wbuf[u])
        whi[u] = w_high
        wlo[u] = w_low
        both = jnp.dot(h2[...], w_high, preferred_element_type=f32)
        rest_part = jnp.dot(h2[pl.ds(0, tokens), :], w_low, preferred_element_type=f32)
        plog[u] = both[:tokens] + both[tokens:] + rest_part
        for i in range(1, n):
            piece(u, i).start()

    forward(v)

    lag = 2
    waited = []
    total = len(order)
    for k in range(total + 2 * lag):
        if k < total:
            i, c = order[k]
            first(i, c).wait_recv()
            if not direct(i, c):
                second(i, c).start()
            beside(0, i, c).start()
        if lag <= k < total + lag:
            i, c = order[k - lag]
            second(i, c).wait_recv()
            beside(1, i, c).start()
        if k >= 2 * lag:
            i, c = order[k - 2 * lag]
            beside(0, i, c).wait_recv()
            beside(1, i, c).wait_recv()
            waited.append(i)
            if waited.count(i) == CHUNKS:
                forward(peers[i])

    token = v * mine + lax.broadcasted_iota(jnp.int32, (mine, 1), 0)
    lane_seq = lax.broadcasted_iota(jnp.int32, (mine, seq), 1)

    def column(ref):
        picked = jnp.zeros((mine, seq), f32)
        for p in range(pairs):
            for s in range(2):
                row = jnp.broadcast_to(ref[p, pl.ds(s, 1), :].astype(f32), (mine, seq))
                picked = jnp.where((token // seq == 2 * p + s) & (token % seq == lane_seq), row, picked)
        return jnp.sum(picked, axis=1, keepdims=True)

    target = column(tgt).astype(jnp.int32)
    outside = column(rest)
    length = jnp.zeros((mine, 1), jnp.int32)
    for p in range(pairs):
        for s in range(2):
            length = jnp.where(token // seq == 2 * p + s, lens[p, s], length)
    live = (token % seq < length).astype(f32)
    lane = lax.broadcasted_iota(jnp.int32, (mine, cols), 1)

    for i in range(1, n):
        remote(rbuf.at[i - 1], rbuf.at[i - 1], rsend.at[i - 1], rrecv.at[i - 1], {"vocab": peers[i]}).wait_recv()
    logits = []
    for u in range(n):
        block = plog[u, pl.ds(pl.multiple_of(v * mine, mine), mine), :]
        for i in range(1, n):
            block = block + rbuf[i - 1, u]
        logits.append(block)
    peak = functools.reduce(jnp.maximum, [jnp.max(b, axis=1, keepdims=True) for b in logits])
    row_total = sum(jnp.sum(jnp.exp(b - peak), axis=1, keepdims=True) for b in logits)
    matches = [target == u * cols + lane for u in range(n)]
    target_logit = sum(
        jnp.sum(jnp.where(k, b, 0.0), axis=1, keepdims=True) for k, b in zip(matches, logits)
    )
    window_lse = peak + jnp.log(row_total)
    ceiling = jnp.maximum(window_lse, outside)
    full_lse = ceiling + jnp.log(jnp.exp(window_lse - ceiling) + jnp.exp(outside - ceiling))
    stat[v] = jnp.broadcast_to((target_logit - full_lse) * live, (mine, LANES))
    for u in range(n):
        gbuf[u, v] = matches[u].astype(f32) - jnp.exp(logits[u] - full_lse)

    def share_stat(i):
        return remote(stat.at[v], stat.at[v], ssend.at[i - 1], srecv.at[i - 1], {"vocab": peers[i]})

    def share_grad(u, i):
        return remote(gbuf.at[u, v], gbuf.at[u, v], gsend.at[u, i - 1], grecv.at[u, i - 1], {"vocab": peers[i]})

    for i in range(1, n):
        share_stat(i).start()
    for u in range(n):
        for i in range(1, n):
            share_grad(u, i).start()

    for i in range(1, n):
        share_stat(i).wait_recv()
    divisor = pairs * sum(gw[g] for g in range(groups))
    position = lax.broadcasted_iota(jnp.int32, (seq, LANES), 0)
    per_token = stat[...].reshape(tokens, LANES)
    local_loss = jnp.zeros((1, LANES), f32)
    scales = []
    for p in range(pairs):
        weight = sum(jnp.where(gmap[p] == g, gw[g], 0.0) for g in range(groups))
        logp = [
            jnp.sum(per_token[(2 * p + s) * seq:(2 * p + s + 1) * seq], axis=0, keepdims=True) for s in range(2)
        ]
        margin = beta_scale * ((logp[0] - refl[p, 0]) - (logp[1] - refl[p, 1]))
        softplus = jnp.maximum(-margin, 0.0) + jnp.log1p(jnp.exp(-jnp.abs(margin)))
        local_loss = local_loss + weight * softplus
        falling = jnp.exp(-jnp.abs(margin))
        sigmoid = jnp.where(margin > 0.0, falling, 1.0) / (1.0 + falling)
        coefficient = -beta_scale * weight * sigmoid / jnp.full((1, LANES), divisor)
        for s in range(2):
            signed = coefficient if s == 0 else -coefficient
            scales.append(jnp.where(position < lens[p, s], jnp.broadcast_to(signed, (seq, LANES)), 0.0))
    lbuf[d] = jnp.broadcast_to(local_loss / jnp.full((1, LANES), divisor), (8, LANES))

    def share_loss(j):
        return remote(lbuf.at[d], lbuf.at[d], dsend, drecv, {"dp": (d + j) % m})

    for j in range(1, m):
        share_loss(j).start()

    contract = (((1,), (1,)), ((), ()))
    for u in range(n):
        for i in range(1, n):
            share_grad(u, i).wait_recv()
        high, low = split(gbuf[u].reshape(tokens, cols))
        part = lax.dot_general(jnp.concatenate([high, low], axis=0), whi[u], contract, preferred_element_type=f32)
        part = part[:tokens] + part[tokens:] + lax.dot_general(high, wlo[u], contract, preferred_element_type=f32)
        if u:
            part = part + out[...]
        if u == n - 1:
            part = part * jnp.concatenate(scales, axis=0)[:, :1]
        out[...] = part

    every_loss = remote(lbuf.at[pl.ds(0, m - 1)], lbuf.at[pl.ds(0, m - 1)], dsend, drecv, partner)
    every_loss.wait_recv()
    summed = lbuf[0]
    for j in range(1, m):
        summed = summed + lbuf[j]
    loss[0, 0] = summed[0, 0]

    for i, c in order:
        first(i, c).wait_send()
        second(i, c).wait_send()
        beside(0, i, c).wait_send()
        beside(1, i, c).wait_send()
    for i in range(1, n):
        remote(rbuf.at[i - 1], rbuf.at[i - 1], rsend.at[i - 1], rrecv.at[i - 1], {"vocab": peers[i]}).wait_send()
        share_stat(i).wait_send()
        for u in range(n):
            share_grad(u, i).wait_send()
    every_loss.wait_send()


def solution(mesh):
    n, m = mesh.shape["vocab"], mesh.shape["dp"]

    def shards(hidden, head_weight, targets, lengths, rest_lse, ref_logp, group_map, group_weight):
        rows = hidden.shape[3]
        tokens = hidden.shape[0] * hidden.shape[1] * hidden.shape[2]
        cols = head_weight.shape[1]
        mine = tokens // n
        vmem, smem = pl.BlockSpec(memory_space=pltpu.VMEM), pl.BlockSpec(memory_space=pltpu.SMEM)
        hbm = pl.BlockSpec(memory_space=pl.ANY)
        dma = pltpu.SemaphoreType.DMA
        grad, loss = pl.pallas_call(
            functools.partial(kernel, n, m),
            out_shape=(jax.ShapeDtypeStruct((tokens, rows), f32), jax.ShapeDtypeStruct((1, 1), f32)),
            in_specs=[hbm, hbm, vmem, smem, vmem, smem, smem, smem],
            out_specs=(vmem, smem),
            scratch_shapes=[
                pltpu.VMEM((tokens, rows), f32),
                pltpu.VMEM((2 * tokens, rows), bf16),
                pltpu.VMEM((n, rows, cols), f32),
                pltpu.VMEM((n, rows, cols), bf16),
                pltpu.VMEM((n, rows, cols), bf16),
                pltpu.VMEM((n, tokens, cols), f32),
                pltpu.VMEM((n - 1, n, mine, cols), f32),
                pltpu.VMEM((n, n, mine, cols), f32),
                pltpu.VMEM((n, mine, LANES), f32),
                pltpu.VMEM((m, 8, LANES), f32),
                dma((2,)),
                dma((n - 1, CHUNKS)), dma((n - 1, CHUNKS)),
                dma((n - 1, CHUNKS)), dma((n - 1, CHUNKS)),
                dma((2, n - 1, CHUNKS)), dma((2, n - 1, CHUNKS)),
                dma((n - 1,)), dma((n - 1,)),
                dma((n, n - 1)), dma((n, n - 1)),
                dma((n - 1,)), dma((n - 1,)),
                dma, dma,
            ],
            compiler_params=pltpu.CompilerParams(
                collective_id=0, has_side_effects=True, vmem_limit_bytes=56 << 20
            ),
        )(hidden.reshape(tokens, rows), head_weight, targets, lengths, rest_lse, ref_logp, group_map, group_weight)
        return grad.reshape(hidden.shape), loss.reshape(())

    return jax.shard_map(
        shards,
        mesh=mesh,
        in_specs=(
            P("dp", None, None, "vocab"),
            P(None, "vocab"),
            P("dp", None, None),
            P("dp", None),
            P("dp", None, None),
            P("dp", None),
            P("dp"),
            P(),
        ),
        out_specs=(P("dp", None, None, "vocab"), P()),
        check_vma=False,
    )
```

```python
import functools

import jax
import jax.numpy as jnp
from jax import lax
from jax.experimental import pallas as pl
from jax.experimental.pallas import tpu as pltpu
from jax.sharding import PartitionSpec as P

beta_scale = 0.05
SHARE = 4
CHUNKS = 4
DIRECT = 2
MESH = pl.DeviceIdType.MESH
f32, bf16 = jnp.float32, jnp.bfloat16
LANES = 128


def split(x):
    high = x.astype(bf16)
    return high, (x - high.astype(f32)).astype(bf16)


def kernel(n, m, hid, w, tgt, lens, rest, refl, gmap, gw, out, loss,
           hbuf, h2, wbuf, whi, wlo, plog, rbuf, gbuf, stat, lbuf,
           lsem, wsend, wrecv, zsend, zrecv, csend, crecv, rsend, rrecv, gsend, grecv, ssend, srecv, dsend, drecv):
    v, d = lax.axis_index("vocab"), lax.axis_index("dp")
    pairs, _, seq = tgt.shape
    tokens, rows = hid.shape
    cols = w.shape[1]
    groups = gw.shape[0]
    mine = tokens // n
    quarter = rows // SHARE
    chunk = quarter // CHUNKS
    share = d % SHARE
    partner = {"dp": d + 1 - 2 * (d % 2)}
    across = {"dp": d + 2 - 4 * ((d // 2) % 2)}
    across_share = (share + 2) % SHARE

    def peer(i):
        u, bit = v, 1
        while bit <= i:
            if i & bit:
                u = u + bit * (1 - 2 * ((v // bit) % 2))
            bit *= 2
        return u

    peers = [peer(i) for i in range(n)]

    def remote(src, dst, ss, rs, where):
        return pltpu.make_async_remote_copy(
            src_ref=src, dst_ref=dst, send_sem=ss, recv_sem=rs, device_id=where, device_id_type=MESH
        )

    barrier = pltpu.get_barrier_semaphore()
    for i in range(1, n):
        pl.semaphore_signal(barrier, inc=1, device_id={"vocab": peers[i]}, device_id_type=MESH)
    for j in range(1, m):
        pl.semaphore_signal(barrier, inc=1, device_id={"dp": (d + j) % m}, device_id_type=MESH)
    own_w = pltpu.make_async_copy(w.at[pl.ds(pl.multiple_of(v * rows, rows), rows), :], wbuf.at[v], lsem.at[0])
    own_h = pltpu.make_async_copy(hid, hbuf, lsem.at[1])
    own_w.start()
    own_h.start()
    pl.semaphore_wait(barrier, n + m - 2)

    def hops(i):
        return bin(i).count("1")

    order = sorted(
        ((i, c) for i in range(1, n) for c in range(CHUNKS)), key=lambda e: (e[1] - hops(e[0]), -hops(e[0]), e[0])
    )

    def direct(i, c):
        return hops(i) == 1 and c >= CHUNKS - DIRECT

    def spot(part, c):
        return pl.ds(pl.multiple_of(part * quarter + c * chunk, chunk), chunk)

    def plane(i, c, part, ss, rs):
        start = pl.multiple_of(peers[i] * rows + part * quarter + c * chunk, chunk)
        return remote(w.at[pl.ds(start, chunk), :], wbuf.at[v, spot(part, c)],
                      ss.at[i - 1, c], rs.at[i - 1, c], {"vocab": peers[i]})

    def first(i, c):
        return plane(i, c, share, wsend, wrecv)

    def second(i, c):
        if direct(i, c):
            return plane(i, c, across_share, zsend, zrecv)
        here = wbuf.at[peers[i], spot(share, c)]
        return remote(here, here, zsend.at[i - 1, c], zrecv.at[i - 1, c], across)

    def beside(kind, i, c):
        here = wbuf.at[peers[i], spot(across_share if kind else share, c)]
        return remote(here, here, csend.at[kind, i - 1, c], crecv.at[kind, i - 1, c], partner)

    for i, c in order:
        first(i, c).start()
        if direct(i, c):
            second(i, c).start()

    own_h.wait()
    high, low = split(hbuf[...])
    h2[pl.ds(0, tokens), :] = high
    h2[pl.ds(tokens, tokens), :] = low
    own_w.wait()

    def piece(u, i):
        return remote(plog.at[u, pl.ds(pl.multiple_of(peers[i] * mine, mine), mine), :], rbuf.at[i - 1, u],
                      rsend.at[i - 1], rrecv.at[i - 1], {"vocab": peers[i]})

    def forward(u):
        w_high, w_low = split(wbuf[u])
        whi[u] = w_high
        wlo[u] = w_low
        both = jnp.dot(h2[...], w_high, preferred_element_type=f32)
        rest_part = jnp.dot(h2[pl.ds(0, tokens), :], w_low, preferred_element_type=f32)
        plog[u] = both[:tokens] + both[tokens:] + rest_part
        for i in reversed(range(1, n)):
            piece(u, i).start()

    forward(v)

    lag = 2
    waited = []
    total = len(order)
    for k in range(total + 2 * lag):
        if k < total:
            i, c = order[k]
            first(i, c).wait_recv()
            if not direct(i, c):
                second(i, c).start()
            beside(0, i, c).start()
        if lag <= k < total + lag:
            i, c = order[k - lag]
            second(i, c).wait_recv()
            beside(1, i, c).start()
        if k >= 2 * lag:
            i, c = order[k - 2 * lag]
            beside(0, i, c).wait_recv()
            beside(1, i, c).wait_recv()
            waited.append(i)
            if waited.count(i) == CHUNKS:
                forward(peers[i])

    token = v * mine + lax.broadcasted_iota(jnp.int32, (mine, 1), 0)
    lane_seq = lax.broadcasted_iota(jnp.int32, (mine, seq), 1)

    def column(ref):
        picked = jnp.zeros((mine, seq), f32)
        for p in range(pairs):
            for s in range(2):
                row = jnp.broadcast_to(ref[p, pl.ds(s, 1), :].astype(f32), (mine, seq))
                picked = jnp.where((token // seq == 2 * p + s) & (token % seq == lane_seq), row, picked)
        return jnp.sum(picked, axis=1, keepdims=True)

    target = column(tgt).astype(jnp.int32)
    outside = column(rest)
    length = jnp.zeros((mine, 1), jnp.int32)
    for p in range(pairs):
        for s in range(2):
            length = jnp.where(token // seq == 2 * p + s, lens[p, s], length)
    live = (token % seq < length).astype(f32)
    lane = lax.broadcasted_iota(jnp.int32, (mine, cols), 1)

    for i in range(1, n):
        remote(rbuf.at[i - 1], rbuf.at[i - 1], rsend.at[i - 1], rrecv.at[i - 1], {"vocab": peers[i]}).wait_recv()
    logits = []
    for u in range(n):
        block = plog[u, pl.ds(pl.multiple_of(v * mine, mine), mine), :]
        for i in range(1, n):
            block = block + rbuf[i - 1, u]
        logits.append(block)
    peak = functools.reduce(jnp.maximum, [jnp.max(b, axis=1, keepdims=True) for b in logits])
    row_total = sum(jnp.sum(jnp.exp(b - peak), axis=1, keepdims=True) for b in logits)
    matches = [target == u * cols + lane for u in range(n)]
    target_logit = sum(
        jnp.sum(jnp.where(k, b, 0.0), axis=1, keepdims=True) for k, b in zip(matches, logits)
    )
    window_lse = peak + jnp.log(row_total)
    ceiling = jnp.maximum(window_lse, outside)
    full_lse = ceiling + jnp.log(jnp.exp(window_lse - ceiling) + jnp.exp(outside - ceiling))
    stat[v] = jnp.broadcast_to((target_logit - full_lse) * live, (mine, LANES))
    for u in range(n):
        gbuf[u, v] = matches[u].astype(f32) - jnp.exp(logits[u] - full_lse)

    def share_stat(i):
        return remote(stat.at[v], stat.at[v], ssend.at[i - 1], srecv.at[i - 1], {"vocab": peers[i]})

    def share_grad(u, i):
        return remote(gbuf.at[u, v], gbuf.at[u, v], gsend.at[u, i - 1], grecv.at[u, i - 1], {"vocab": peers[i]})

    for i in range(1, n):
        share_stat(i).start()
    for u in range(n):
        for i in reversed(range(1, n)):
            share_grad(u, i).start()

    for i in range(1, n):
        share_stat(i).wait_recv()
    divisor = pairs * sum(gw[g] for g in range(groups))
    position = lax.broadcasted_iota(jnp.int32, (seq, LANES), 0)
    per_token = stat[...].reshape(tokens, LANES)
    local_loss = jnp.zeros((1, LANES), f32)
    scales = []
    for p in range(pairs):
        weight = sum(jnp.where(gmap[p] == g, gw[g], 0.0) for g in range(groups))
        logp = [
            jnp.sum(per_token[(2 * p + s) * seq:(2 * p + s + 1) * seq], axis=0, keepdims=True) for s in range(2)
        ]
        margin = beta_scale * ((logp[0] - refl[p, 0]) - (logp[1] - refl[p, 1]))
        softplus = jnp.maximum(-margin, 0.0) + jnp.log1p(jnp.exp(-jnp.abs(margin)))
        local_loss = local_loss + weight * softplus
        falling = jnp.exp(-jnp.abs(margin))
        sigmoid = jnp.where(margin > 0.0, falling, 1.0) / (1.0 + falling)
        coefficient = -beta_scale * weight * sigmoid / jnp.full((1, LANES), divisor)
        for s in range(2):
            signed = coefficient if s == 0 else -coefficient
            scales.append(jnp.where(position < lens[p, s], jnp.broadcast_to(signed, (seq, LANES)), 0.0))
    lbuf[d] = jnp.broadcast_to(local_loss / jnp.full((1, LANES), divisor), (8, LANES))

    def share_loss(j):
        return remote(lbuf.at[d], lbuf.at[d], dsend, drecv, {"dp": (d + j) % m})

    for j in range(1, m):
        share_loss(j).start()

    contract = (((1,), (1,)), ((), ()))
    for u in range(n):
        for i in range(1, n):
            share_grad(u, i).wait_recv()
        high, low = split(gbuf[u].reshape(tokens, cols))
        part = lax.dot_general(jnp.concatenate([high, low], axis=0), whi[u], contract, preferred_element_type=f32)
        part = part[:tokens] + part[tokens:] + lax.dot_general(high, wlo[u], contract, preferred_element_type=f32)
        if u:
            part = part + out[...]
        if u == n - 1:
            part = part * jnp.concatenate(scales, axis=0)[:, :1]
        out[...] = part

    every_loss = remote(lbuf.at[pl.ds(0, m - 1)], lbuf.at[pl.ds(0, m - 1)], dsend, drecv, partner)
    every_loss.wait_recv()
    summed = lbuf[0]
    for j in range(1, m):
        summed = summed + lbuf[j]
    loss[0, 0] = summed[0, 0]

    for i, c in order:
        first(i, c).wait_send()
        second(i, c).wait_send()
        beside(0, i, c).wait_send()
        beside(1, i, c).wait_send()
    for i in range(1, n):
        remote(rbuf.at[i - 1], rbuf.at[i - 1], rsend.at[i - 1], rrecv.at[i - 1], {"vocab": peers[i]}).wait_send()
        share_stat(i).wait_send()
        for u in range(n):
            share_grad(u, i).wait_send()
    every_loss.wait_send()


def solution(mesh):
    n, m = mesh.shape["vocab"], mesh.shape["dp"]

    def shards(hidden, head_weight, targets, lengths, rest_lse, ref_logp, group_map, group_weight):
        rows = hidden.shape[3]
        tokens = hidden.shape[0] * hidden.shape[1] * hidden.shape[2]
        cols = head_weight.shape[1]
        mine = tokens // n
        vmem, smem = pl.BlockSpec(memory_space=pltpu.VMEM), pl.BlockSpec(memory_space=pltpu.SMEM)
        hbm = pl.BlockSpec(memory_space=pl.ANY)
        dma = pltpu.SemaphoreType.DMA
        grad, loss = pl.pallas_call(
            functools.partial(kernel, n, m),
            out_shape=(jax.ShapeDtypeStruct((tokens, rows), f32), jax.ShapeDtypeStruct((1, 1), f32)),
            in_specs=[hbm, hbm, vmem, smem, vmem, smem, smem, smem],
            out_specs=(vmem, smem),
            scratch_shapes=[
                pltpu.VMEM((tokens, rows), f32),
                pltpu.VMEM((2 * tokens, rows), bf16),
                pltpu.VMEM((n, rows, cols), f32),
                pltpu.VMEM((n, rows, cols), bf16),
                pltpu.VMEM((n, rows, cols), bf16),
                pltpu.VMEM((n, tokens, cols), f32),
                pltpu.VMEM((n - 1, n, mine, cols), f32),
                pltpu.VMEM((n, n, mine, cols), f32),
                pltpu.VMEM((n, mine, LANES), f32),
                pltpu.VMEM((m, 8, LANES), f32),
                dma((2,)),
                dma((n - 1, CHUNKS)), dma((n - 1, CHUNKS)),
                dma((n - 1, CHUNKS)), dma((n - 1, CHUNKS)),
                dma((2, n - 1, CHUNKS)), dma((2, n - 1, CHUNKS)),
                dma((n - 1,)), dma((n - 1,)),
                dma((n, n - 1)), dma((n, n - 1)),
                dma((n - 1,)), dma((n - 1,)),
                dma, dma,
            ],
            compiler_params=pltpu.CompilerParams(
                collective_id=0, has_side_effects=True, vmem_limit_bytes=56 << 20
            ),
        )(hidden.reshape(tokens, rows), head_weight, targets, lengths, rest_lse, ref_logp, group_map, group_weight)
        return grad.reshape(hidden.shape), loss.reshape(())

    return jax.shard_map(
        shards,
        mesh=mesh,
        in_specs=(
            P("dp", None, None, "vocab"),
            P(None, "vocab"),
            P("dp", None, None),
            P("dp", None),
            P("dp", None, None),
            P("dp", None),
            P("dp"),
            P(),
        ),
        out_specs=(P("dp", None, None, "vocab"), P()),
        check_vma=False,
    )
```
